512 devices in a mesh: pipe: 16 (over y, z_lo), expert: 32 (over z_hi, x, core).
Axes of the slice: x: 4, y: 8, z: 8 (z_hi: 4, z_lo: 2; z = z_hi * 2 + z_lo), core: 2. Of those that a mesh axis runs over, the one named last changes fastest.
Arguments:
- in_flight: bfloat16 [2, 16, 512, 3584], P(None, 'pipe', 'expert'), may hold values from -6 to 6
- norm_gain: bfloat16 [2, 16, 3584], P(None, 'pipe'), may hold values from 0.099609375 to 1.8984375
- router_weight: bfloat16 [2, 16, 3584, 4], P(None, 'pipe'), may hold values from -0.09375 to 0.09375
- up_weight: bfloat16 [2, 16, 3584, 4096], P(None, 'pipe', None, 'expert'), may hold values from -0.09375 to 0.09375
- down_weight: bfloat16 [2, 16, 4096, 3584], P(None, 'pipe', 'expert'), may hold values from -0.1875 to 0.1875
- chosen_experts: int32 [1, 2, 16, 512, 2], P(None, None, 'pipe', 'expert'), may hold values from 0 to 3, all different within a row; in each aligned block of 16 rows (0 to 15, 16 to 31, ..., all dimensions but the last counted through in order) at most 14 rows name the same one
Outputs:
- final_states: bfloat16 [2, 16, 512, 3584], P(None, 'pipe', 'expert')
The draws below stay inside these ranges and needn't reach their ends.
Inputs may be any that keep to these rules, and one draw needn't show every extreme that they name: `chosen_experts`: each token names 2 different experts; among the tokens of one device's rows of one micro-batch at one step, at most 14 name the same expert, and that most is reached.
All inputs are finite; a program needn't handle non-finite values.
Results may differ from the reference program's by a relative error of at most 0.006.
Values may be sent and summed in bfloat16 or wider, within the bound.
A program may use at most 64 MiB of HBM per device.

```python
import math
import jax
import jax.numpy as jnp
import numpy as np
from jax import lax

D = 3584
HID = 1024
EXPERTS = 4
TOPK = 2
ROWS = 16
TICKS = 1
GROUP = 8
HID_DEV = 128
TOKENS = 512
N_PIPE = 16


def steps_of(key, extent, split, low, high):
    level, own = 1.0, jax.random.fold_in(key, 6)
    for dim, blocks in split:
        heights = jnp.exp(jax.random.uniform(jax.random.fold_in(own, dim), (blocks,), jnp.float32, low / len(split), high / len(split)))
        level = level * jnp.repeat(heights, extent[dim] // blocks).reshape([-1 if axis == dim else 1 for axis in range(len(extent))])
    return level


def shared_out(rng, own, number, rows, count, top, bound, lean):
    ranking = jax.random.permutation(rng, count)
    packed, usual = load_shares(count, rows * top, bound, lean, True), load_shares(count, rows * top, bound, lean, False)
    places = jnp.arange(count)

    def named(tallies, turn):
        used = int((tallies > 0).sum())
        fixed = max(1, used // 4)
        shifted = fixed + (places - fixed + turn * (used - fixed)) % max(1, count - fixed)
        return jnp.zeros((count,), jnp.int32).at[ranking[jnp.where(places < fixed, places, shifted)]].set(jnp.asarray(tallies, jnp.int32))

    tallies = jnp.where(number % 4 == 0, named(packed, number // 4), named(usual, number - number // 4 - 1))
    mixed = jax.random.permutation(jax.random.fold_in(own, 3), count)
    donor, sink = mixed[0:count // 2 * 2:2], mixed[1:count // 2 * 2:2]
    room = jnp.minimum(tallies[donor] - 1, bound - tallies[sink]) // 2
    room = jnp.where((donor == ranking[0]) | (sink == ranking[0]) | (tallies[sink] == 0), 0, jnp.maximum(room, 0))
    shifted = jax.random.randint(jax.random.fold_in(own, 4), (count // 2,), 0, 1 << 20) % (room + 1)
    tallies = tallies.at[donor].add(-shifted).at[sink].add(shifted)
    items = jnp.searchsorted(jnp.cumsum(tallies), jnp.arange(rows * top), side="right").astype(jnp.int32)
    table = items.reshape(top, rows).T
    table = table[jax.random.permutation(jax.random.fold_in(own, 1), rows)]
    turn = jax.random.randint(jax.random.fold_in(own, 2), (rows, 1), 0, top)
    return jnp.take_along_axis(table, (jnp.arange(top)[None, :] + turn) % top, axis=1)


def load_shares(number_of, total, reach, skew, full):
    loads = [(1 << 20) // math.isqrt(standing ** skew) + 1 for standing in range(1, number_of + 1)]
    largest = reach if full else min(reach, max(-(-total // number_of), total * loads[0] // sum(loads)))
    least = 1 if total - largest >= number_of - 1 else 0
    given, rest = [largest] + [least] * (number_of - 1), total - largest - least * (number_of - 1)
    while rest > 0:
        free = [i for i in range(1, number_of) if given[i] < largest] or [i for i in range(1, number_of) if given[i] < reach]
        mass, remaining = sum([loads[i] for i in free]), rest
        for i in free:
            extra = min(reach - given[i], max(1, remaining * loads[i] // mass), rest)
            given[i] = given[i] + extra
            rest = rest - extra
    return np.array(given)


def gaussian(rng, extent, width, most, shards=(), kind=jnp.bfloat16):
    result = width * jax.random.normal(rng, extent, jnp.float32)
    if shards:
        result = result * steps_of(rng, extent, shards, -0.22, 0.18)
    return jnp.clip(result, -most, most).astype(kind)


def setup_inputs(seed: int = 0) -> dict:
    key_list = jax.random.split(jax.random.key(seed), 7)
    in_flight = gaussian(key_list[0], (2, N_PIPE, TOKENS, D), 1.0, 6.0, ((1, 16), (2, 32)))
    norm_gain = jnp.clip(1.0 + 0.18 * jax.random.normal(key_list[1], (2, N_PIPE, D), jnp.float32), 0.099609375, 1.8984375).astype(jnp.bfloat16)
    router_weight = gaussian(key_list[2], (2, N_PIPE, D, EXPERTS), D ** -0.5, 0.09375, ((1, 16),))
    up_weight = gaussian(key_list[3], (2, N_PIPE, D, EXPERTS * HID), D ** -0.5, 0.09375, ((1, 16), (3, 32)))
    down_weight = gaussian(key_list[4], (2, N_PIPE, EXPERTS * HID, D), HID ** -0.5, 0.1875, ((1, 16), (2, 32)))
    chosen_experts_keys = jax.random.split(jax.random.fold_in(key_list[5], 1), TICKS * 2 * N_PIPE * TOKENS // ROWS)
    chosen_experts_turns = jax.random.permutation(jax.random.fold_in(key_list[5], 3), TICKS * 2 * N_PIPE * TOKENS // ROWS)
    chosen_experts = jax.vmap(lambda own, number: shared_out(jax.random.fold_in(key_list[5], 2), own, number, ROWS, EXPERTS, TOPK, ROWS * 7 // 8, 1))(chosen_experts_keys, chosen_experts_turns).reshape((TICKS, 2, N_PIPE, TOKENS, TOPK))
    return {"in_flight": in_flight, "norm_gain": norm_gain, "router_weight": router_weight, "up_weight": up_weight, "down_weight": down_weight, "chosen_experts": chosen_experts}


def layer_apply(inputs):
    tokens, gain, router, w_up, w_down, chosen = inputs
    wide = tokens.astype(jnp.float32)
    scale = lax.rsqrt(lax.optimization_barrier(jnp.mean(wide * wide, axis=-1, keepdims=True)) + 1e-06)
    normed = (wide * scale * gain.astype(jnp.float32)).astype(jnp.bfloat16)
    affinity = jax.nn.sigmoid(jnp.dot(normed, router, preferred_element_type=jnp.float32))
    labels = jnp.arange(EXPERTS, dtype=jnp.int32)
    picked = lax.optimization_barrier(jnp.sum((chosen[:, :, None] == labels[None, None, :]).astype(jnp.float32), axis=1))
    weighted = affinity * picked
    gates = weighted / lax.optimization_barrier(jnp.sum(weighted, axis=-1, keepdims=True))
    total = wide
    for expert in range(EXPERTS):
        hidden = jax.nn.silu(jnp.dot(normed, w_up[:, expert * HID:(expert + 1) * HID], preferred_element_type=jnp.float32)).astype(jnp.bfloat16)
        blocks = hidden.reshape(hidden.shape[0], GROUP, HID_DEV).astype(jnp.float32)
        down_rows = w_down[expert * HID:(expert + 1) * HID].reshape(GROUP, HID_DEV, D).astype(jnp.float32)
        partial_value = jnp.einsum('tgh,ghd->tgd', blocks, down_rows).astype(jnp.bfloat16)
        total = total + gates[:, expert:expert + 1] * lax.optimization_barrier(jnp.sum(partial_value.astype(jnp.float32), axis=1))
    return total.astype(jnp.bfloat16)

def reference(in_flight, norm_gain, router_weight, up_weight, down_weight, chosen_experts):
    states = in_flight
    for tick in range(TICKS):
        flat = (states.reshape(2 * N_PIPE, TOKENS, D), norm_gain.reshape(2 * N_PIPE, D), router_weight.reshape(2 * N_PIPE, D, EXPERTS), up_weight.reshape(2 * N_PIPE, D, EXPERTS * HID), down_weight.reshape(2 * N_PIPE, EXPERTS * HID, D), chosen_experts[tick].reshape(2 * N_PIPE, TOKENS, TOPK))
        moved = lax.map(layer_apply, flat).reshape(2, N_PIPE, TOKENS, D)
        down_leg = jnp.concatenate([moved[1, :1], moved[0, :-1]], axis=0)
        up_leg = jnp.concatenate([moved[1, 1:], moved[0, -1:]], axis=0)
        states = jnp.stack([down_leg, up_leg])
    return states
```

```python
import jax
import jax.numpy as jnp
from jax import lax
from jax.sharding import PartitionSpec as P

EXPERTS = 4


def from_behind(value, axis, by):
    size = lax.axis_size(axis)
    pairs = [(i, i + by) for i in range(size) if 0 <= i + by < size]
    return lax.ppermute(value, axis, pairs)


def shards(in_flight, norm_gain, router_weight, up_weight, down_weight, chosen_experts):
    pipe_rank = lax.axis_index("pipe")
    last_rank = lax.axis_size("pipe") - 1
    devices = lax.axis_size("expert")
    group = lax.axis_index("expert") // (devices // EXPERTS)
    wide = in_flight[:, 0].astype(jnp.float32)
    legs, rows, width = wide.shape
    scale = lax.rsqrt(jnp.mean(wide * wide, axis=-1, keepdims=True) + 1e-06)
    normed = (wide * scale * norm_gain.astype(jnp.float32)).astype(jnp.bfloat16)
    affinity = jax.nn.sigmoid(
        jnp.einsum("lrd,lde->lre", normed, router_weight[:, 0], preferred_element_type=jnp.float32)
    )
    labels = jnp.arange(EXPERTS, dtype=jnp.int32)
    picked = jnp.sum(
        (chosen_experts[0, :, 0, :, :, None] == labels).astype(jnp.float32), axis=2
    )
    weighted = affinity * picked
    gates = weighted / jnp.sum(weighted, axis=-1, keepdims=True)
    gates = jnp.pad(gates, ((0, 0), (0, 0), (0, 128 - EXPERTS)))
    everyone = lax.all_gather(normed, "expert", axis=1, tiled=True)
    gates = lax.all_gather(gates, "expert", axis=1, tiled=True)
    gate = jnp.sum(jnp.where(jnp.arange(128) == group, gates, 0.0), axis=-1, keepdims=True)
    hidden = jnp.einsum(
        "lkd,ldh->lkh", everyone, up_weight[:, 0], preferred_element_type=jnp.float32
    )
    hidden = (jax.nn.silu(hidden) * gate).astype(jnp.bfloat16)
    partial = jnp.einsum(
        "lkh,lhd->lkd", hidden, down_weight[:, 0], preferred_element_type=jnp.float32
    ).astype(jnp.bfloat16)
    moe = lax.psum_scatter(partial, "expert", scatter_dimension=1, tiled=True)
    moved = (wide + moe.astype(jnp.float32)).astype(jnp.bfloat16)
    first_out, second_out = moved[0], moved[1]
    from_above = from_behind(first_out, "pipe", 1)
    from_below = from_behind(second_out, "pipe", -1)
    states = [
        jnp.where(pipe_rank == 0, second_out, from_above),
        jnp.where(pipe_rank == last_rank, first_out, from_below),
    ]
    return jnp.stack(states)[:, None]


def solution(mesh):
    in_specs = (
        P(None, "pipe", "expert", None),
        P(None, "pipe", None),
        P(None, "pipe", None, None),
        P(None, "pipe", None, "expert"),
        P(None, "pipe", "expert", None),
        P(None, None, "pipe", "expert", None),
    )
    out_specs = P(None, "pipe", "expert", None)
    return jax.shard_map(shards, mesh=mesh, in_specs=in_specs, out_specs=out_specs, check_vma=False)
```

```python
import jax
import jax.numpy as jnp
from jax import lax
from jax.experimental import pallas as pl
from jax.experimental.pallas import tpu as pltpu
from jax.sharding import PartitionSpec as P

EXPERTS = 4
RING = 4
CORES = 2
LEGS = 2
LANES = 128
TILE = 512
ORDER = (2, 1, 3, 0)


def from_behind(value, axis, by):
    size = lax.axis_size(axis)
    pairs = [(i, i + by) for i in range(size) if 0 <= i + by < size]
    return lax.ppermute(value, axis, pairs)


def kernel(own, wide, up_hbm, down_hbm, out, rows_in, part, near, early, late, zearly, zlate,
           up, down, send, recv, local):
    width = out.shape[-1]
    me = lax.axis_index("expert")
    z, x, c = me // (RING * CORES), (me // CORES) % RING, me % CORES

    def at(zz, xx, cc):
        return (zz * RING + xx) * CORES + cc

    def turn(v, by):
        return (v + by) % RING

    zp, zm = at(turn(z, 1), x, c), at(turn(z, 3), x, c)
    xp, xm = at(z, turn(x, 1), c), at(z, turn(x, 3), c)
    sib = at(z, x, 1 - c)

    weights = [
        pltpu.make_async_copy(up_hbm, up, local.at[0]),
        pltpu.make_async_copy(down_hbm, down, local.at[1]),
    ]
    for copy in weights:
        copy.start()

    barrier = pltpu.get_barrier_semaphore()
    for device in (zp, zm, xp, xm, sib):
        pl.semaphore_signal(
            barrier, inc=1, device_id={"expert": device}, device_id_type=pl.DeviceIdType.MESH
        )
    pl.semaphore_wait(barrier, 5)

    started = {}

    def go(name, src, dst, device):
        number = len(started)
        copy = pltpu.make_async_remote_copy(
            src_ref=src,
            dst_ref=dst,
            send_sem=send.at[number],
            recv_sem=recv.at[number],
            device_id={"expert": device},
            device_id_type=pl.DeviceIdType.MESH,
        )
        copy.start()
        started[name] = copy

    def got(*name):
        started[name].wait_recv()

    def slot(dx, dz):
        return rows_in.at[turn(x, dx), c, turn(z, dz)]

    def spread(dz):
        src = own if dz == 0 else slot(0, dz)
        go(("x1p", dz), src, slot(0, dz), xp)
        go(("x1m", dz), src, slot(0, dz), xm)
        go(("c", 0, dz), src, slot(0, dz), sib)

    def relay(dz):
        got("x1p", dz)
        go(("x2p", dz), slot(3, dz).at[0], slot(3, dz).at[0], xp)
        go(("c", 3, dz), slot(3, dz), slot(3, dz), sib)
        got("x1m", dz)
        go(("x2m", dz), slot(1, dz).at[1], slot(1, dz).at[1], xm)
        go(("c", 1, dz), slot(1, dz), slot(1, dz), sib)

    def finish(dz):
        got("x2p", dz)
        go(("c2p", dz), slot(2, dz).at[0], slot(2, dz).at[0], sib)
        got("x2m", dz)
        go(("c2m", dz), slot(2, dz).at[1], slot(2, dz).at[1], sib)

    def compute(dx):
        xx = turn(x, dx)

        def leg_body(leg, carry):
            lhs = rows_in[xx, :, :, leg]
            flat = lhs.reshape(CORES * RING * lhs.shape[2], lhs.shape[3])
            lane = lax.broadcasted_iota(jnp.int32, (1, LANES), 1)
            mine = (lane == z) | (lane == z + EXPERTS)
            gate = jnp.sum(
                jnp.where(mine, flat[:, width:].astype(jnp.float32), 0.0), axis=1, keepdims=True
            )
            hidden = jnp.dot(flat[:, :width], up[leg], preferred_element_type=jnp.float32)
            hidden = (hidden / (1.0 + jnp.exp(-hidden)) * gate).astype(jnp.bfloat16)

            def tile_body(tile, carry):
                columns = pl.ds(pl.multiple_of(tile * TILE, TILE), TILE)
                value = jnp.dot(hidden, down[leg, :, columns], preferred_element_type=jnp.float32)
                part[xx, :, :, leg, :, columns] = value.astype(jnp.bfloat16).reshape(
                    CORES, RING, lhs.shape[2], TILE
                )
                return carry

            return lax.fori_loop(0, width // TILE, tile_body, carry)

        lax.fori_loop(0, LEGS, leg_body, 0)
        go(("near", dx), part.at[xx, 1 - c], near.at[dx], sib)

    def pair(dx):
        got("near", dx)
        xx = turn(x, dx)

        def body(zz, carry):
            total = part[xx, c, zz].astype(jnp.float32) + near[dx, zz].astype(jnp.float32)
            part[xx, c, zz] = total.astype(jnp.bfloat16)
            return carry

        lax.fori_loop(0, RING, body, 0)

    def mine(dx, dz, leg):
        return part.at[turn(x, dx), c, turn(z, dz), leg]

    def add(ref, other):
        ref[...] = (ref[...].astype(jnp.float32) + other[...].astype(jnp.float32)).astype(
            jnp.bfloat16
        )

    go(("z1p",), own, slot(0, 0), zp)
    go(("z1m",), own, slot(0, 0), zm)
    spread(0)
    rows_in[x, c, z] = own[...]
    got("z1p")
    go(("z2p",), slot(0, 3).at[0], slot(0, 3).at[0], zp)
    spread(3)
    got("z1m")
    go(("z2m",), slot(0, 1).at[1], slot(0, 1).at[1], zm)
    spread(1)
    relay(0)
    got("z2p")
    got("z2m")
    spread(2)
    for copy in weights:
        copy.wait()
    relay(3)
    relay(1)
    for dz in (0, 3, 1, 2):
        got("c", 0, dz)
    compute(0)
    relay(2)
    for dz in (0, 3, 1, 2):
        got("c", 3, dz)
    for dz in (0, 3, 1, 2):
        got("c", 1, dz)
    finish(0)
    compute(1)
    finish(3)
    compute(3)
    pair(1)
    for dz in ORDER:
        go(("late", 1, dz), mine(1, dz, 1), late.at[0, turn(z, dz), 1], xp)
    pair(3)
    for dz in ORDER:
        go(("late", 0, dz), mine(3, dz, 0), late.at[1, turn(z, dz), 0], xm)
    finish(1)
    finish(2)
    for dz in (0, 3, 1, 2):
        got("c2p", dz)
        got("c2m", dz)
    compute(2)
    pair(0)
    pair(2)
    for dz in ORDER:
        go(("early", 0, dz), mine(2, dz, 0), early.at[0, turn(z, dz)], xp)
        go(("early", 1, dz), mine(2, dz, 1), early.at[1, turn(z, dz)], xm)
    for dz in ORDER:
        got("early", 0, dz)
        add(mine(1, dz, 0), early.at[0, turn(z, dz)])
        go(("late", 2, dz), mine(1, dz, 0), late.at[0, turn(z, dz), 0], xp)
        got("early", 1, dz)
        add(mine(3, dz, 1), early.at[1, turn(z, dz)])
        go(("late", 3, dz), mine(3, dz, 1), late.at[1, turn(z, dz), 1], xm)

    def settle(dz):
        for number in range(4):
            got("late", number, dz)
        zz = turn(z, dz)
        total = part[x, c, zz].astype(jnp.float32) + late[0, zz].astype(jnp.float32)
        part[x, c, zz] = (total + late[1, zz].astype(jnp.float32)).astype(jnp.bfloat16)

    settle(2)
    go(("zearly", 0), mine(0, 2, 0), zearly.at[0], zp)
    go(("zearly", 1), mine(0, 2, 1), zearly.at[1], zm)
    settle(1)
    go(("zlate", 0), mine(0, 1, 1), zlate.at[0, 1], zp)
    settle(3)
    go(("zlate", 1), mine(0, 3, 0), zlate.at[1, 0], zm)
    got("zearly", 0)
    add(mine(0, 1, 0), zearly.at[0])
    go(("zlate", 2), mine(0, 1, 0), zlate.at[0, 0], zp)
    got("zearly", 1)
    add(mine(0, 3, 1), zearly.at[1])
    go(("zlate", 3), mine(0, 3, 1), zlate.at[1, 1], zm)
    settle(0)
    for number in range(4):
        got("zlate", number)
    total = wide[...].astype(jnp.float32) + part[x, c, z].astype(jnp.float32)
    total = total + zlate[0].astype(jnp.float32) + zlate[1].astype(jnp.float32)
    out[...] = total.astype(out.dtype)
    for copy in started.values():
        copy.wait_send()


def experts(packed, tokens, up, down):
    legs, rows, wide = packed.shape
    width = tokens.shape[2]
    vmem = pl.BlockSpec(memory_space=pltpu.VMEM)
    anywhere = pl.BlockSpec(memory_space=pl.ANY)
    copies = 88
    return pl.pallas_call(
        kernel,
        out_shape=jax.ShapeDtypeStruct(tokens.shape, jnp.bfloat16),
        in_specs=[vmem, vmem, anywhere, anywhere],
        out_specs=vmem,
        scratch_shapes=[
            pltpu.VMEM((RING, CORES, RING, legs, rows, wide), jnp.bfloat16),
            pltpu.VMEM((RING, CORES, RING, legs, rows, width), jnp.bfloat16),
            pltpu.VMEM((RING, RING, legs, rows, width), jnp.bfloat16),
            pltpu.VMEM((2, RING, rows, width), jnp.bfloat16),
            pltpu.VMEM((2, RING, legs, rows, width), jnp.bfloat16),
            pltpu.VMEM((2, rows, width), jnp.bfloat16),
            pltpu.VMEM((2, legs, rows, width), jnp.bfloat16),
            pltpu.VMEM(up.shape, up.dtype),
            pltpu.VMEM(down.shape, down.dtype),
            pltpu.SemaphoreType.DMA((copies,)),
            pltpu.SemaphoreType.DMA((copies,)),
            pltpu.SemaphoreType.DMA((2,)),
        ],
        compiler_params=pltpu.CompilerParams(
            collective_id=0, has_side_effects=True, vmem_limit_bytes=48 * 1024 * 1024
        ),
        name="experts",
    )(packed, tokens, up, down)


def shards(in_flight, norm_gain, router_weight, up_weight, down_weight, chosen_experts):
    pipe_rank = lax.axis_index("pipe")
    last_rank = lax.axis_size("pipe") - 1
    tokens = in_flight[:, 0]
    wide = tokens.astype(jnp.float32)
    scale = lax.rsqrt(jnp.mean(wide * wide, axis=-1, keepdims=True) + 1e-06)
    normed = (wide * scale * norm_gain.astype(jnp.float32)).astype(jnp.bfloat16)
    affinity = jax.nn.sigmoid(
        jnp.einsum("lrd,lde->lre", normed, router_weight[:, 0], preferred_element_type=jnp.float32)
    )
    labels = jnp.arange(EXPERTS, dtype=jnp.int32)
    picked = jnp.sum(
        (chosen_experts[0, :, 0, :, :, None] == labels).astype(jnp.float32), axis=2
    )
    weighted = affinity * picked
    gates = weighted / jnp.sum(weighted, axis=-1, keepdims=True)
    high = gates.astype(jnp.bfloat16)
    low = (gates - high.astype(jnp.float32)).astype(jnp.bfloat16)
    empty = jnp.zeros(gates.shape[:2] + (LANES - 2 * EXPERTS,), jnp.bfloat16)
    packed = jnp.concatenate([normed, high, low, empty], axis=-1)
    moved = experts(packed, tokens, up_weight[:, 0], down_weight[:, 0])
    first_out, second_out = moved[0], moved[1]
    from_above = from_behind(first_out, "pipe", 1)
    from_below = from_behind(second_out, "pipe", -1)
    states = [
        jnp.where(pipe_rank == 0, second_out, from_above),
        jnp.where(pipe_rank == last_rank, first_out, from_below),
    ]
    return jnp.stack(states)[:, None]


def solution(mesh):
    in_specs = (
        P(None, "pipe", "expert", None),
        P(None, "pipe", None),
        P(None, "pipe", None, None),
        P(None, "pipe", None, "expert"),
        P(None, "pipe", "expert", None),
        P(None, None, "pipe", "expert", None),
    )
    out_specs = P(None, "pipe", "expert", None)
    return jax.shard_map(shards, mesh=mesh, in_specs=in_specs, out_specs=out_specs, check_vma=False)
```

```python
import jax
import jax.numpy as jnp
from jax import lax
from jax.experimental import pallas as pl
from jax.experimental.pallas import tpu as pltpu
from jax.sharding import PartitionSpec as P

EXPERTS = 4
RING = 4
CORES = 2
LEGS = 2
LANES = 128
TILE = 512
ORDER = (2, 1, 3, 0)


def kernel(own, wide, up_hbm, down_hbm, out, rows_in, part, near, early, late, zearly, zlate,
           moved, arrived, up, down, send, recv, local,
           pipe_send, pipe_recv):
    width = out.shape[-1]
    me = lax.axis_index("expert")
    z, x, c = me // (RING * CORES), (me // CORES) % RING, me % CORES

    def at(zz, xx, cc):
        return (zz * RING + xx) * CORES + cc

    def turn(v, by):
        return (v + by) % RING

    zp, zm = at(turn(z, 1), x, c), at(turn(z, 3), x, c)
    xp, xm = at(z, turn(x, 1), c), at(z, turn(x, 3), c)
    sib = at(z, x, 1 - c)

    weights = [
        pltpu.make_async_copy(up_hbm, up, local.at[0]),
        pltpu.make_async_copy(down_hbm, down, local.at[1]),
    ]
    for copy in weights:
        copy.start()

    barrier = pltpu.get_barrier_semaphore()
    for device in (zp, zm, xp, xm, sib):
        pl.semaphore_signal(
            barrier, inc=1, device_id={"expert": device}, device_id_type=pl.DeviceIdType.MESH
        )
    rank, ranks = lax.axis_index("pipe"), lax.axis_size("pipe")
    above, below = (rank + 1) % ranks, (rank + ranks - 1) % ranks
    for device in (above, below):
        pl.semaphore_signal(
            barrier, inc=1, device_id={"pipe": device}, device_id_type=pl.DeviceIdType.MESH
        )
    pl.semaphore_wait(barrier, 7)

    started = {}

    def go(name, src, dst, device):
        number = len(started)
        copy = pltpu.make_async_remote_copy(
            src_ref=src,
            dst_ref=dst,
            send_sem=send.at[number],
            recv_sem=recv.at[number],
            device_id={"expert": device},
            device_id_type=pl.DeviceIdType.MESH,
        )
        copy.start()
        started[name] = copy

    def got(*name):
        started[name].wait_recv()

    def slot(dx, dz):
        return rows_in.at[turn(x, dx), c, turn(z, dz)]

    def spread(dz):
        src = own if dz == 0 else slot(0, dz)
        go(("x1p", dz), src, slot(0, dz), xp)
        go(("x1m", dz), src, slot(0, dz), xm)
        go(("c", 0, dz), src, slot(0, dz), sib)

    def relay(dz):
        got("x1p", dz)
        go(("x2p", dz), slot(3, dz).at[0], slot(3, dz).at[0], xp)
        go(("c", 3, dz), slot(3, dz), slot(3, dz), sib)
        got("x1m", dz)
        go(("x2m", dz), slot(1, dz).at[1], slot(1, dz).at[1], xm)
        go(("c", 1, dz), slot(1, dz), slot(1, dz), sib)

    def finish(dz):
        got("x2p", dz)
        go(("c2p", dz), slot(2, dz).at[0], slot(2, dz).at[0], sib)
        got("x2m", dz)
        go(("c2m", dz), slot(2, dz).at[1], slot(2, dz).at[1], sib)

    def compute(dx):
        xx = turn(x, dx)

        def leg_body(leg, carry):
            lhs = rows_in[xx, :, :, leg]
            flat = lhs.reshape(CORES * RING * lhs.shape[2], lhs.shape[3])
            lane = lax.broadcasted_iota(jnp.int32, (1, LANES), 1)
            mine = (lane == z) | (lane == z + EXPERTS)
            gate = jnp.sum(
                jnp.where(mine, flat[:, width:].astype(jnp.float32), 0.0), axis=1, keepdims=True
            )
            hidden = jnp.dot(flat[:, :width], up[leg], preferred_element_type=jnp.float32)
            hidden = (hidden / (1.0 + jnp.exp(-hidden)) * gate).astype(jnp.bfloat16)

            def tile_body(tile, carry):
                columns = pl.ds(pl.multiple_of(tile * TILE, TILE), TILE)
                value = jnp.dot(hidden, down[leg, :, columns], preferred_element_type=jnp.float32)
                part[xx, :, :, leg, :, columns] = value.astype(jnp.bfloat16).reshape(
                    CORES, RING, lhs.shape[2], TILE
                )
                return carry

            return lax.fori_loop(0, width // TILE, tile_body, carry)

        lax.fori_loop(0, LEGS, leg_body, 0)
        go(("near", dx), part.at[xx, 1 - c], near.at[dx], sib)

    def pair(dx):
        got("near", dx)
        xx = turn(x, dx)

        def body(zz, carry):
            total = part[xx, c, zz].astype(jnp.float32) + near[dx, zz].astype(jnp.float32)
            part[xx, c, zz] = total.astype(jnp.bfloat16)
            return carry

        lax.fori_loop(0, RING, body, 0)

    def mine(dx, dz, leg):
        return part.at[turn(x, dx), c, turn(z, dz), leg]

    def add(ref, other):
        ref[...] = (ref[...].astype(jnp.float32) + other[...].astype(jnp.float32)).astype(
            jnp.bfloat16
        )

    go(("z1p",), own, slot(0, 0), zp)
    go(("z1m",), own, slot(0, 0), zm)
    spread(0)
    rows_in[x, c, z] = own[...]
    got("z1p")
    go(("z2p",), slot(0, 3).at[0], slot(0, 3).at[0], zp)
    spread(3)
    got("z1m")
    go(("z2m",), slot(0, 1).at[1], slot(0, 1).at[1], zm)
    spread(1)
    relay(0)
    got("z2p")
    got("z2m")
    spread(2)
    for copy in weights:
        copy.wait()
    relay(3)
    relay(1)
    for dz in (0, 3, 1, 2):
        got("c", 0, dz)
    compute(0)
    relay(2)
    for dz in (0, 3, 1, 2):
        got("c", 3, dz)
    for dz in (0, 3, 1, 2):
        got("c", 1, dz)
    finish(0)
    compute(1)
    finish(3)
    compute(3)
    pair(1)
    for dz in ORDER:
        go(("late", 1, dz), mine(1, dz, 1), late.at[0, turn(z, dz), 1], xp)
    pair(3)
    for dz in ORDER:
        go(("late", 0, dz), mine(3, dz, 0), late.at[1, turn(z, dz), 0], xm)
    finish(1)
    finish(2)
    for dz in (0, 3, 1, 2):
        got("c2p", dz)
        got("c2m", dz)
    compute(2)
    pair(0)
    pair(2)
    def depart(dz):
        go(("early", 0, dz), mine(2, dz, 0), early.at[0, turn(z, dz)], xp)
        go(("early", 1, dz), mine(2, dz, 1), early.at[1, turn(z, dz)], xm)

    def onward(dz):
        got("early", 0, dz)
        add(mine(1, dz, 0), early.at[0, turn(z, dz)])
        go(("late", 2, dz), mine(1, dz, 0), late.at[0, turn(z, dz), 0], xp)
        got("early", 1, dz)
        add(mine(3, dz, 1), early.at[1, turn(z, dz)])
        go(("late", 3, dz), mine(3, dz, 1), late.at[1, turn(z, dz), 1], xm)

    def settle(dz):
        for number in range(4):
            got("late", number, dz)
        zz = turn(z, dz)
        total = part[x, c, zz].astype(jnp.float32) + late[0, zz].astype(jnp.float32)
        part[x, c, zz] = (total + late[1, zz].astype(jnp.float32)).astype(jnp.bfloat16)

    depart(2)
    depart(1)
    depart(3)
    onward(2)
    depart(0)
    onward(1)
    onward(3)
    settle(2)
    go(("zearly", 0), mine(0, 2, 0), zearly.at[0], zp)
    go(("zearly", 1), mine(0, 2, 1), zearly.at[1], zm)
    onward(0)
    settle(1)
    go(("zlate", 0), mine(0, 1, 1), zlate.at[0, 1], zp)
    settle(3)
    go(("zlate", 1), mine(0, 3, 0), zlate.at[1, 0], zm)
    got("zearly", 0)
    add(mine(0, 1, 0), zearly.at[0])
    go(("zlate", 2), mine(0, 1, 0), zlate.at[0, 0], zp)
    got("zearly", 1)
    add(mine(0, 3, 1), zearly.at[1])
    go(("zlate", 3), mine(0, 3, 1), zlate.at[1, 1], zm)
    settle(0)
    last = ranks - 1

    def hand(leg, device):
        return pltpu.make_async_remote_copy(
            src_ref=moved.at[leg],
            dst_ref=arrived.at[leg],
            send_sem=pipe_send.at[leg],
            recv_sem=pipe_recv.at[leg],
            device_id={"pipe": device},
            device_id_type=pl.DeviceIdType.MESH,
        )

    first, second = hand(0, above), hand(1, below)

    def total(leg):
        value = wide[leg].astype(jnp.float32) + part[x, c, z, leg].astype(jnp.float32)
        value = value + zlate[0, leg].astype(jnp.float32) + zlate[1, leg].astype(jnp.float32)
        moved[leg] = value.astype(jnp.bfloat16)

    got("zlate", 1)
    got("zlate", 2)
    total(0)
    pl.when(rank < last)(first.start)
    got("zlate", 0)
    got("zlate", 3)
    total(1)
    pl.when(rank > 0)(second.start)

    @pl.when(rank == 0)
    def _():
        out[0] = moved[1]

    @pl.when(rank == last)
    def _():
        out[1] = moved[0]

    @pl.when(rank > 0)
    def _():
        first.wait_recv()
        out[0] = arrived[0]

    @pl.when(rank < last)
    def _():
        second.wait_recv()
        out[1] = arrived[1]

    pl.when(rank < last)(first.wait_send)
    pl.when(rank > 0)(second.wait_send)
    for copy in started.values():
        copy.wait_send()


def experts(packed, tokens, up, down):
    legs, rows, wide = packed.shape
    width = tokens.shape[2]
    vmem = pl.BlockSpec(memory_space=pltpu.VMEM)
    anywhere = pl.BlockSpec(memory_space=pl.ANY)
    copies = 88
    return pl.pallas_call(
        kernel,
        out_shape=jax.ShapeDtypeStruct(tokens.shape, jnp.bfloat16),
        in_specs=[vmem, vmem, anywhere, anywhere],
        out_specs=vmem,
        scratch_shapes=[
            pltpu.VMEM((RING, CORES, RING, legs, rows, wide), jnp.bfloat16),
            pltpu.VMEM((RING, CORES, RING, legs, rows, width), jnp.bfloat16),
            pltpu.VMEM((RING, RING, legs, rows, width), jnp.bfloat16),
            pltpu.VMEM((2, RING, rows, width), jnp.bfloat16),
            pltpu.VMEM((2, RING, legs, rows, width), jnp.bfloat16),
            pltpu.VMEM((2, rows, width), jnp.bfloat16),
            pltpu.VMEM((2, legs, rows, width), jnp.bfloat16),
            pltpu.VMEM(tokens.shape, jnp.bfloat16),
            pltpu.VMEM(tokens.shape, jnp.bfloat16),
            pltpu.VMEM(up.shape, up.dtype),
            pltpu.VMEM(down.shape, down.dtype),
            pltpu.SemaphoreType.DMA((copies,)),
            pltpu.SemaphoreType.DMA((copies,)),
            pltpu.SemaphoreType.DMA((2,)),
            pltpu.SemaphoreType.DMA((2,)),
            pltpu.SemaphoreType.DMA((2,)),
        ],
        compiler_params=pltpu.CompilerParams(
            collective_id=0, has_side_effects=True, vmem_limit_bytes=66000000
        ),
        name="experts",
    )(packed, tokens, up, down)


def shards(in_flight, norm_gain, router_weight, up_weight, down_weight, chosen_experts):
    tokens = in_flight[:, 0]
    wide = tokens.astype(jnp.float32)
    scale = lax.rsqrt(jnp.mean(wide * wide, axis=-1, keepdims=True) + 1e-06)
    normed = (wide * scale * norm_gain.astype(jnp.float32)).astype(jnp.bfloat16)
    affinity = jax.nn.sigmoid(
        jnp.einsum("lrd,lde->lre", normed, router_weight[:, 0], preferred_element_type=jnp.float32)
    )
    labels = jnp.arange(EXPERTS, dtype=jnp.int32)
    picked = jnp.sum(
        (chosen_experts[0, :, 0, :, :, None] == labels).astype(jnp.float32), axis=2
    )
    weighted = affinity * picked
    gates = weighted / jnp.sum(weighted, axis=-1, keepdims=True)
    high = gates.astype(jnp.bfloat16)
    low = (gates - high.astype(jnp.float32)).astype(jnp.bfloat16)
    empty = jnp.zeros(gates.shape[:2] + (LANES - 2 * EXPERTS,), jnp.bfloat16)
    packed = jnp.concatenate([normed, high, low, empty], axis=-1)
    return experts(packed, tokens, up_weight[:, 0], down_weight[:, 0])[:, None]


def solution(mesh):
    in_specs = (
        P(None, "pipe", "expert", None),
        P(None, "pipe", None),
        P(None, "pipe", None, None),
        P(None, "pipe", None, "expert"),
        P(None, "pipe", "expert", None),
        P(None, None, "pipe", "expert", None),
    )
    out_specs = P(None, "pipe", "expert", None)
    return jax.shard_map(shards, mesh=mesh, in_specs=in_specs, out_specs=out_specs, check_vma=False)
```

```python
import jax
import jax.numpy as jnp
from jax import lax
from jax.experimental import pallas as pl
from jax.experimental.pallas import tpu as pltpu
from jax.sharding import PartitionSpec as P

EXPERTS = 4
RING = 4
CORES = 2
LEGS = 2
LANES = 128
TILE = 512
ORDER = (2, 1, 3, 0)


def kernel(wide, gain, router, chosen, up_hbm, down_hbm, moved, out, own, rows_in, part, near, early, late, zearly, zlate,
           arrived, up, down, send, recv, local,
           pipe_send, pipe_recv):
    width = out.shape[-1]
    me = lax.axis_index("expert")
    z, x, c = me // (RING * CORES), (me // CORES) % RING, me % CORES

    def at(zz, xx, cc):
        return (zz * RING + xx) * CORES + cc

    def turn(v, by):
        return (v + by) % RING

    zp, zm = at(turn(z, 1), x, c), at(turn(z, 3), x, c)
    xp, xm = at(z, turn(x, 1), c), at(z, turn(x, 3), c)
    sib = at(z, x, 1 - c)

    weights = [
        pltpu.make_async_copy(up_hbm, up, local.at[0]),
        pltpu.make_async_copy(down_hbm, down, local.at[1]),
    ]
    for copy in weights:
        copy.start()

    barrier = pltpu.get_barrier_semaphore()
    for device in (zp, zm, xp, xm, sib):
        pl.semaphore_signal(
            barrier, inc=1, device_id={"expert": device}, device_id_type=pl.DeviceIdType.MESH
        )
    rank, ranks = lax.axis_index("pipe"), lax.axis_size("pipe")
    above, below = (rank + 1) % ranks, (rank + ranks - 1) % ranks
    for device in (above, below):
        pl.semaphore_signal(
            barrier, inc=1, device_id={"pipe": device}, device_id_type=pl.DeviceIdType.MESH
        )

    lane = lax.broadcasted_iota(jnp.int32, (1, LANES), 1)
    label = lane % EXPERTS
    for leg in range(LEGS):
        value = wide[leg].astype(jnp.float32)
        scale = lax.rsqrt(jnp.mean(value * value, axis=-1, keepdims=True) + 1e-06)
        normed = (value * scale * gain[...].astype(jnp.float32)[leg : leg + 1]).astype(jnp.bfloat16)
        own[leg, :, :width] = normed
        normed = normed.astype(jnp.float32)
        logits = jnp.zeros((normed.shape[0], LANES), jnp.float32)
        for expert in range(EXPERTS):
            column = router[leg, expert : expert + 1].astype(jnp.float32)
            logit = jnp.sum(normed * column, axis=-1, keepdims=True)
            logits = jnp.where(label == expert, logit, logits)
        named = (chosen[leg, :, 0:1] == label) | (chosen[leg, :, 1:2] == label)
        weighted = jnp.where(named, jax.nn.sigmoid(logits), 0.0)
        first_four = jnp.where(lane < EXPERTS, weighted, 0.0)
        gates = weighted / jnp.sum(first_four, axis=-1, keepdims=True)
        high = gates.astype(jnp.bfloat16).astype(jnp.float32)
        gates = jnp.where(lane < EXPERTS, high, jnp.where(lane < 2 * EXPERTS, gates - high, 0.0))
        own[leg, :, width:] = gates.astype(jnp.bfloat16)

    pl.semaphore_wait(barrier, 7)

    started = {}

    def go(name, src, dst, device):
        number = len(started)
        copy = pltpu.make_async_remote_copy(
            src_ref=src,
            dst_ref=dst,
            send_sem=send.at[number],
            recv_sem=recv.at[number],
            device_id={"expert": device},
            device_id_type=pl.DeviceIdType.MESH,
        )
        copy.start()
        started[name] = copy

    def got(*name):
        started[name].wait_recv()

    def slot(dx, dz):
        return rows_in.at[turn(x, dx), c, turn(z, dz)]

    def spread(dz):
        src = own if dz == 0 else slot(0, dz)
        go(("x1p", dz), src, slot(0, dz), xp)
        go(("x1m", dz), src, slot(0, dz), xm)
        go(("c", 0, dz), src, slot(0, dz), sib)

    def relay(dz):
        got("x1p", dz)
        go(("x2p", dz), slot(3, dz).at[0], slot(3, dz).at[0], xp)
        go(("c", 3, dz), slot(3, dz), slot(3, dz), sib)
        got("x1m", dz)
        go(("x2m", dz), slot(1, dz).at[1], slot(1, dz).at[1], xm)
        go(("c", 1, dz), slot(1, dz), slot(1, dz), sib)

    def finish(dz):
        got("x2p", dz)
        go(("c2p", dz), slot(2, dz).at[0], slot(2, dz).at[0], sib)
        got("x2m", dz)
        go(("c2m", dz), slot(2, dz).at[1], slot(2, dz).at[1], sib)

    def compute(dx):
        xx = turn(x, dx)

        def leg_body(leg, carry):
            lhs = rows_in[xx, :, :, leg]
            flat = lhs.reshape(CORES * RING * lhs.shape[2], lhs.shape[3])
            lane = lax.broadcasted_iota(jnp.int32, (1, LANES), 1)
            mine = (lane == z) | (lane == z + EXPERTS)
            gate = jnp.sum(
                jnp.where(mine, flat[:, width:].astype(jnp.float32), 0.0), axis=1, keepdims=True
            )
            hidden = jnp.dot(flat[:, :width], up[leg], preferred_element_type=jnp.float32)
            hidden = (hidden / (1.0 + jnp.exp(-hidden)) * gate).astype(jnp.bfloat16)

            def tile_body(tile, carry):
                columns = pl.ds(pl.multiple_of(tile * TILE, TILE), TILE)
                value = jnp.dot(hidden, down[leg, :, columns], preferred_element_type=jnp.float32)
                part[xx, :, :, leg, :, columns] = value.astype(jnp.bfloat16).reshape(
                    CORES, RING, lhs.shape[2], TILE
                )
                return carry

            return lax.fori_loop(0, width // TILE, tile_body, carry)

        lax.fori_loop(0, LEGS, leg_body, 0)
        go(("near", dx), part.at[xx, 1 - c], near.at[dx], sib)

    def pair(dx):
        got("near", dx)
        xx = turn(x, dx)

        def body(zz, carry):
            total = part[xx, c, zz].astype(jnp.float32) + near[dx, zz].astype(jnp.float32)
            part[xx, c, zz] = total.astype(jnp.bfloat16)
            return carry

        lax.fori_loop(0, RING, body, 0)

    def mine(dx, dz, leg):
        return part.at[turn(x, dx), c, turn(z, dz), leg]

    def add(ref, other):
        ref[...] = (ref[...].astype(jnp.float32) + other[...].astype(jnp.float32)).astype(
            jnp.bfloat16
        )

    go(("z1p",), own, slot(0, 0), zp)
    go(("z1m",), own, slot(0, 0), zm)
    spread(0)
    rows_in[x, c, z] = own[...]
    got("z1p")
    go(("z2p",), slot(0, 3).at[0], slot(0, 3).at[0], zp)
    spread(3)
    got("z1m")
    go(("z2m",), slot(0, 1).at[1], slot(0, 1).at[1], zm)
    spread(1)
    relay(0)
    got("z2p")
    got("z2m")
    spread(2)
    for copy in weights:
        copy.wait()
    relay(3)
    relay(1)
    for dz in (0, 3, 1, 2):
        got("c", 0, dz)
    compute(0)
    relay(2)
    for dz in (0, 3, 1, 2):
        got("c", 3, dz)
    for dz in (0, 3, 1, 2):
        got("c", 1, dz)
    finish(0)
    compute(1)
    finish(3)
    compute(3)
    pair(1)
    for dz in ORDER:
        go(("late", 1, dz), mine(1, dz, 1), late.at[0, turn(z, dz), 1], xp)
    pair(3)
    for dz in ORDER:
        go(("late", 0, dz), mine(3, dz, 0), late.at[1, turn(z, dz), 0], xm)
    finish(1)
    finish(2)
    for dz in (0, 3, 1, 2):
        got("c2p", dz)
        got("c2m", dz)
    compute(2)
    pair(0)
    pair(2)
    def depart(dz):
        go(("early", 0, dz), mine(2, dz, 0), early.at[0, turn(z, dz)], xp)
        go(("early", 1, dz), mine(2, dz, 1), early.at[1, turn(z, dz)], xm)

    def onward(dz):
        got("early", 0, dz)
        add(mine(1, dz, 0), early.at[0, turn(z, dz)])
        go(("late", 2, dz), mine(1, dz, 0), late.at[0, turn(z, dz), 0], xp)
        got("early", 1, dz)
        add(mine(3, dz, 1), early.at[1, turn(z, dz)])
        go(("late", 3, dz), mine(3, dz, 1), late.at[1, turn(z, dz), 1], xm)

    def settle(dz):
        for number in range(4):
            got("late", number, dz)
        zz = turn(z, dz)
        total = part[x, c, zz].astype(jnp.float32) + late[0, zz].astype(jnp.float32)
        part[x, c, zz] = (total + late[1, zz].astype(jnp.float32)).astype(jnp.bfloat16)

    depart(2)
    depart(1)
    depart(3)
    onward(2)
    depart(0)
    onward(1)
    onward(3)
    settle(2)
    go(("zearly", 0), mine(0, 2, 0), zearly.at[0], zp)
    go(("zearly", 1), mine(0, 2, 1), zearly.at[1], zm)
    onward(0)
    settle(1)
    go(("zlate", 0), mine(0, 1, 1), zlate.at[0, 1], zp)
    settle(3)
    go(("zlate", 1), mine(0, 3, 0), zlate.at[1, 0], zm)
    got("zearly", 0)
    add(mine(0, 1, 0), zearly.at[0])
    go(("zlate", 2), mine(0, 1, 0), zlate.at[0, 0], zp)
    got("zearly", 1)
    add(mine(0, 3, 1), zearly.at[1])
    go(("zlate", 3), mine(0, 3, 1), zlate.at[1, 1], zm)
    settle(0)
    last = ranks - 1

    def hand(leg, device):
        return pltpu.make_async_remote_copy(
            src_ref=moved.at[leg],
            dst_ref=arrived.at[leg],
            send_sem=pipe_send.at[leg],
            recv_sem=pipe_recv.at[leg],
            device_id={"pipe": device},
            device_id_type=pl.DeviceIdType.MESH,
        )

    first, second = hand(0, above), hand(1, below)

    def total(leg):
        value = wide[leg].astype(jnp.float32) + part[x, c, z, leg].astype(jnp.float32)
        value = value + zlate[0, leg].astype(jnp.float32) + zlate[1, leg].astype(jnp.float32)
        moved[leg] = value.astype(jnp.bfloat16)

    got("zlate", 1)
    got("zlate", 2)
    total(0)
    pl.when(rank < last)(first.start)
    got("zlate", 0)
    got("zlate", 3)
    total(1)
    pl.when(rank > 0)(second.start)

    @pl.when(rank == 0)
    def _():
        out[0] = jnp.zeros(out.shape[1:], out.dtype)

    @pl.when(rank == last)
    def _():
        out[1] = jnp.zeros(out.shape[1:], out.dtype)

    @pl.when(rank > 0)
    def _():
        first.wait_recv()
        out[0] = arrived[0]

    @pl.when(rank < last)
    def _():
        second.wait_recv()
        out[1] = arrived[1]

    pl.when(rank < last)(first.wait_send)
    pl.when(rank > 0)(second.wait_send)
    for copy in started.values():
        copy.wait_send()


def experts(tokens, gain, router, chosen, up, down):
    legs, rows, width = tokens.shape
    wide = width + LANES
    vmem = pl.BlockSpec(memory_space=pltpu.VMEM)
    anywhere = pl.BlockSpec(memory_space=pl.ANY)
    copies = 88
    return pl.pallas_call(
        kernel,
        out_shape=[jax.ShapeDtypeStruct(tokens.shape, jnp.bfloat16)] * 2,
        in_specs=[vmem, vmem, vmem, vmem, anywhere, anywhere],
        out_specs=[vmem, vmem],
        scratch_shapes=[
            pltpu.VMEM((legs, rows, wide), jnp.bfloat16),
            pltpu.VMEM((RING, CORES, RING, legs, rows, wide), jnp.bfloat16),
            pltpu.VMEM((RING, CORES, RING, legs, rows, width), jnp.bfloat16),
            pltpu.VMEM((RING, RING, legs, rows, width), jnp.bfloat16),
            pltpu.VMEM((2, RING, rows, width), jnp.bfloat16),
            pltpu.VMEM((2, RING, legs, rows, width), jnp.bfloat16),
            pltpu.VMEM((2, rows, width), jnp.bfloat16),
            pltpu.VMEM((2, legs, rows, width), jnp.bfloat16),
            pltpu.VMEM(tokens.shape, jnp.bfloat16),
            pltpu.VMEM(up.shape, up.dtype),
            pltpu.VMEM(down.shape, down.dtype),
            pltpu.SemaphoreType.DMA((copies,)),
            pltpu.SemaphoreType.DMA((copies,)),
            pltpu.SemaphoreType.DMA((2,)),
            pltpu.SemaphoreType.DMA((2,)),
            pltpu.SemaphoreType.DMA((2,)),
        ],
        compiler_params=pltpu.CompilerParams(
            collective_id=0, has_side_effects=True, vmem_limit_bytes=66000000
        ),
        name="experts",
    )(tokens, gain, router, chosen, up, down)


def shards(in_flight, norm_gain, router_weight, up_weight, down_weight, chosen_experts):
    rank, ranks = lax.axis_index("pipe"), lax.axis_size("pipe")
    moved, arrived = experts(
        in_flight[:, 0],
        norm_gain[:, 0],
        router_weight[:, 0].transpose(0, 2, 1),
        chosen_experts[0, :, 0],
        up_weight[:, 0],
        down_weight[:, 0],
    )
    states = [
        jnp.where(rank == 0, moved[1], arrived[0]),
        jnp.where(rank == ranks - 1, moved[0], arrived[1]),
    ]
    return jnp.stack(states)[:, None]


def solution(mesh):
    in_specs = (
        P(None, "pipe", "expert", None),
        P(None, "pipe", None),
        P(None, "pipe", None, None),
        P(None, "pipe", None, "expert"),
        P(None, "pipe", "expert", None),
        P(None, None, "pipe", "expert", None),
    )
    out_specs = P(None, "pipe", "expert", None)
    return jax.shard_map(shards, mesh=mesh, in_specs=in_specs, out_specs=out_specs, check_vma=False)
```

```python
import jax
import jax.numpy as jnp
from jax import lax
from jax.experimental import pallas as pl
from jax.experimental.pallas import tpu as pltpu
from jax.sharding import PartitionSpec as P

EXPERTS = 4
RING = 4
CORES = 2
LEGS = 2
LANES = 128
TILE = 512
ORDER = (2, 1, 3, 0)


def kernel(wide, gain, router, chosen, up_hbm, down_hbm, moved, out, own, rows_in, part, near, early, late, zearly, zlate,
           arrived, up, down, send, recv, local,
           pipe_send, pipe_recv):
    width = out.shape[-1]
    me = lax.axis_index("expert")
    z, x, c = me // (RING * CORES), (me // CORES) % RING, me % CORES

    def at(zz, xx, cc):
        return (zz * RING + xx) * CORES + cc

    def turn(v, by):
        return (v + by) % RING

    zp, zm = at(turn(z, 1), x, c), at(turn(z, 3), x, c)
    xp, xm = at(z, turn(x, 1), c), at(z, turn(x, 3), c)
    sib = at(z, x, 1 - c)

    weights = [
        pltpu.make_async_copy(up_hbm, up, local.at[0]),
        pltpu.make_async_copy(down_hbm, down, local.at[1]),
    ]
    for copy in weights:
        copy.start()

    barrier = pltpu.get_barrier_semaphore()
    for device in (zp, zm, xp, xm, sib):
        pl.semaphore_signal(
            barrier, inc=1, device_id={"expert": device}, device_id_type=pl.DeviceIdType.MESH
        )
    rank, ranks = lax.axis_index("pipe"), lax.axis_size("pipe")
    above, below = (rank + 1) % ranks, (rank + ranks - 1) % ranks
    for device in (above, below):
        pl.semaphore_signal(
            barrier, inc=1, device_id={"pipe": device}, device_id_type=pl.DeviceIdType.MESH
        )

    lane = lax.broadcasted_iota(jnp.int32, (1, LANES), 1)
    label = lane % EXPERTS
    for leg in range(LEGS):
        value = wide[leg].astype(jnp.float32)
        scale = lax.rsqrt(jnp.mean(value * value, axis=-1, keepdims=True) + 1e-06)
        normed = (value * scale * gain[...].astype(jnp.float32)[leg : leg + 1]).astype(jnp.bfloat16)
        own[leg, :, :width] = normed
        normed = normed.astype(jnp.float32)
        logits = jnp.zeros((normed.shape[0], LANES), jnp.float32)
        for expert in range(EXPERTS):
            column = router[leg, expert : expert + 1].astype(jnp.float32)
            logit = jnp.sum(normed * column, axis=-1, keepdims=True)
            logits = jnp.where(label == expert, logit, logits)
        named = (chosen[leg, :, 0:1] == label) | (chosen[leg, :, 1:2] == label)
        weighted = jnp.where(named, jax.nn.sigmoid(logits), 0.0)
        first_four = jnp.where(lane < EXPERTS, weighted, 0.0)
        gates = weighted / jnp.sum(first_four, axis=-1, keepdims=True)
        high = gates.astype(jnp.bfloat16).astype(jnp.float32)
        gates = jnp.where(lane < EXPERTS, high, jnp.where(lane < 2 * EXPERTS, gates - high, 0.0))
        own[leg, :, width:] = gates.astype(jnp.bfloat16)

    pl.semaphore_wait(barrier, 7)

    started = {}

    def go(name, src, dst, device):
        number = len(started)
        copy = pltpu.make_async_remote_copy(
            src_ref=src,
            dst_ref=dst,
            send_sem=send.at[number],
            recv_sem=recv.at[number],
            device_id={"expert": device},
            device_id_type=pl.DeviceIdType.MESH,
        )
        copy.start()
        started[name] = copy

    def got(*name):
        started[name].wait_recv()

    def slot(dx, dz):
        return rows_in.at[turn(x, dx), c, turn(z, dz)]

    def spread(dz):
        src = own if dz == 0 else slot(0, dz)
        go(("x1p", dz), src, slot(0, dz), xp)
        go(("x1m", dz), src, slot(0, dz), xm)
        go(("c", 0, dz), src, slot(0, dz), sib)

    def relay(dz):
        got("x1p", dz)
        go(("x2p", dz), slot(3, dz).at[0], slot(3, dz).at[0], xp)
        go(("c", 3, dz), slot(3, dz), slot(3, dz), sib)
        got("x1m", dz)
        go(("x2m", dz), slot(1, dz).at[1], slot(1, dz).at[1], xm)
        go(("c", 1, dz), slot(1, dz), slot(1, dz), sib)

    def finish(dz):
        got("x2p", dz)
        go(("c2p", dz), slot(2, dz).at[0], slot(2, dz).at[0], sib)
        got("x2m", dz)
        go(("c2m", dz), slot(2, dz).at[1], slot(2, dz).at[1], sib)

    def compute(dx):
        xx = turn(x, dx)

        def leg_body(leg, carry):
            lhs = rows_in[xx, :, :, leg]
            flat = lhs.reshape(CORES * RING * lhs.shape[2], lhs.shape[3])
            lane = lax.broadcasted_iota(jnp.int32, (1, LANES), 1)
            mine = (lane == z) | (lane == z + EXPERTS)
            gate = jnp.sum(
                jnp.where(mine, flat[:, width:].astype(jnp.float32), 0.0), axis=1, keepdims=True
            )
            hidden = jnp.dot(flat[:, :width], up[leg], preferred_element_type=jnp.float32)
            hidden = (hidden / (1.0 + jnp.exp(-hidden)) * gate).astype(jnp.bfloat16)

            def tile_body(tile, carry):
                columns = pl.ds(pl.multiple_of(tile * TILE, TILE), TILE)
                value = jnp.dot(hidden, down[leg, :, columns], preferred_element_type=jnp.float32)
                part[xx, :, :, leg, :, columns] = value.astype(jnp.bfloat16).reshape(
                    CORES, RING, lhs.shape[2], TILE
                )
                return carry

            return lax.fori_loop(0, width // TILE, tile_body, carry)

        for leg in range(LEGS):
            leg_body(leg, 0)
            go(("near", dx, leg), part.at[xx, 1 - c, :, leg], near.at[dx, :, leg], sib)

    def pair(dx):
        got("near", dx, 0)
        got("near", dx, 1)
        xx = turn(x, dx)

        def body(zz, carry):
            total = part[xx, c, zz].astype(jnp.float32) + near[dx, zz].astype(jnp.float32)
            part[xx, c, zz] = total.astype(jnp.bfloat16)
            return carry

        lax.fori_loop(0, RING, body, 0)

    def mine(dx, dz, leg):
        return part.at[turn(x, dx), c, turn(z, dz), leg]

    def add(ref, other):
        ref[...] = (ref[...].astype(jnp.float32) + other[...].astype(jnp.float32)).astype(
            jnp.bfloat16
        )

    go(("z1p",), own, slot(0, 0), zp)
    go(("z1m",), own, slot(0, 0), zm)
    spread(0)
    rows_in[x, c, z] = own[...]
    got("z1p")
    go(("z2p",), slot(0, 3).at[0], slot(0, 3).at[0], zp)
    spread(3)
    got("z1m")
    go(("z2m",), slot(0, 1).at[1], slot(0, 1).at[1], zm)
    spread(1)
    relay(0)
    got("z2p")
    got("z2m")
    spread(2)
    for copy in weights:
        copy.wait()
    relay(3)
    relay(1)
    for dz in (0, 3, 1, 2):
        got("c", 0, dz)
    compute(0)
    relay(2)
    for dz in (0, 3, 1, 2):
        got("c", 3, dz)
    for dz in (0, 3, 1, 2):
        got("c", 1, dz)
    finish(0)
    compute(1)
    finish(3)
    compute(3)
    pair(1)
    for dz in ORDER:
        go(("late", 1, dz), mine(1, dz, 1), late.at[0, turn(z, dz), 1], xp)
    pair(3)
    for dz in ORDER:
        go(("late", 0, dz), mine(3, dz, 0), late.at[1, turn(z, dz), 0], xm)
    finish(1)
    finish(2)
    for dz in (0, 3, 1, 2):
        got("c2p", dz)
        got("c2m", dz)
    compute(2)
    pair(0)
    pair(2)
    def depart(dz):
        go(("early", 0, dz), mine(2, dz, 0), early.at[0, turn(z, dz)], xp)
        go(("early", 1, dz), mine(2, dz, 1), early.at[1, turn(z, dz)], xm)

    def onward(dz):
        got("early", 0, dz)
        add(mine(1, dz, 0), early.at[0, turn(z, dz)])
        go(("late", 2, dz), mine(1, dz, 0), late.at[0, turn(z, dz), 0], xp)
        got("early", 1, dz)
        add(mine(3, dz, 1), early.at[1, turn(z, dz)])
        go(("late", 3, dz), mine(3, dz, 1), late.at[1, turn(z, dz), 1], xm)

    def settle(dz):
        for number in range(4):
            got("late", number, dz)
        zz = turn(z, dz)
        total = part[x, c, zz].astype(jnp.float32) + late[0, zz].astype(jnp.float32)
        part[x, c, zz] = (total + late[1, zz].astype(jnp.float32)).astype(jnp.bfloat16)

    depart(2)
    depart(1)
    depart(3)
    onward(2)
    depart(0)
    onward(1)
    onward(3)
    settle(2)
    go(("zearly", 0), mine(0, 2, 0), zearly.at[0], zp)
    go(("zearly", 1), mine(0, 2, 1), zearly.at[1], zm)
    onward(0)
    settle(1)
    go(("zlate", 0), mine(0, 1, 1), zlate.at[0, 1], zp)
    settle(3)
    go(("zlate", 1), mine(0, 3, 0), zlate.at[1, 0], zm)
    got("zearly", 0)
    add(mine(0, 1, 0), zearly.at[0])
    go(("zlate", 2), mine(0, 1, 0), zlate.at[0, 0], zp)
    got("zearly", 1)
    add(mine(0, 3, 1), zearly.at[1])
    go(("zlate", 3), mine(0, 3, 1), zlate.at[1, 1], zm)
    settle(0)
    last = ranks - 1

    def hand(leg, device):
        return pltpu.make_async_remote_copy(
            src_ref=moved.at[leg],
            dst_ref=arrived.at[leg],
            send_sem=pipe_send.at[leg],
            recv_sem=pipe_recv.at[leg],
            device_id={"pipe": device},
            device_id_type=pl.DeviceIdType.MESH,
        )

    first, second = hand(0, above), hand(1, below)

    def total(leg):
        value = wide[leg].astype(jnp.float32) + part[x, c, z, leg].astype(jnp.float32)
        value = value + zlate[0, leg].astype(jnp.float32) + zlate[1, leg].astype(jnp.float32)
        moved[leg] = value.astype(jnp.bfloat16)

    got("zlate", 1)
    got("zlate", 2)
    total(0)
    pl.when(rank < last)(first.start)
    got("zlate", 0)
    got("zlate", 3)
    total(1)
    pl.when(rank > 0)(second.start)

    @pl.when(rank == 0)
    def _():
        out[0] = jnp.zeros(out.shape[1:], out.dtype)

    @pl.when(rank == last)
    def _():
        out[1] = jnp.zeros(out.shape[1:], out.dtype)

    @pl.when(rank > 0)
    def _():
        first.wait_recv()
        out[0] = arrived[0]

    @pl.when(rank < last)
    def _():
        second.wait_recv()
        out[1] = arrived[1]

    pl.when(rank < last)(first.wait_send)
    pl.when(rank > 0)(second.wait_send)
    for copy in started.values():
        copy.wait_send()


def experts(tokens, gain, router, chosen, up, down):
    legs, rows, width = tokens.shape
    wide = width + LANES
    vmem = pl.BlockSpec(memory_space=pltpu.VMEM)
    anywhere = pl.BlockSpec(memory_space=pl.ANY)
    copies = 88
    return pl.pallas_call(
        kernel,
        out_shape=[jax.ShapeDtypeStruct(tokens.shape, jnp.bfloat16)] * 2,
        in_specs=[vmem, vmem, vmem, vmem, anywhere, anywhere],
        out_specs=[vmem, vmem],
        scratch_shapes=[
            pltpu.VMEM((legs, rows, wide), jnp.bfloat16),
            pltpu.VMEM((RING, CORES, RING, legs, rows, wide), jnp.bfloat16),
            pltpu.VMEM((RING, CORES, RING, legs, rows, width), jnp.bfloat16),
            pltpu.VMEM((RING, RING, legs, rows, width), jnp.bfloat16),
            pltpu.VMEM((2, RING, rows, width), jnp.bfloat16),
            pltpu.VMEM((2, RING, legs, rows, width), jnp.bfloat16),
            pltpu.VMEM((2, rows, width), jnp.bfloat16),
            pltpu.VMEM((2, legs, rows, width), jnp.bfloat16),
            pltpu.VMEM(tokens.shape, jnp.bfloat16),
            pltpu.VMEM(up.shape, up.dtype),
            pltpu.VMEM(down.shape, down.dtype),
            pltpu.SemaphoreType.DMA((copies,)),
            pltpu.SemaphoreType.DMA((copies,)),
            pltpu.SemaphoreType.DMA((2,)),
            pltpu.SemaphoreType.DMA((2,)),
            pltpu.SemaphoreType.DMA((2,)),
        ],
        compiler_params=pltpu.CompilerParams(
            collective_id=0, has_side_effects=True, vmem_limit_bytes=66000000
        ),
        name="experts",
    )(tokens, gain, router, chosen, up, down)


def shards(in_flight, norm_gain, router_weight, up_weight, down_weight, chosen_experts):
    rank, ranks = lax.axis_index("pipe"), lax.axis_size("pipe")
    moved, arrived = experts(
        in_flight[:, 0],
        norm_gain[:, 0],
        router_weight[:, 0].transpose(0, 2, 1),
        chosen_experts[0, :, 0],
        up_weight[:, 0],
        down_weight[:, 0],
    )
    edge = jnp.stack([rank == 0, rank == ranks - 1])[:, None, None]
    return jnp.where(edge, moved[::-1], arrived)[:, None]


def solution(mesh):
    in_specs = (
        P(None, "pipe", "expert", None),
        P(None, "pipe", None),
        P(None, "pipe", None, None),
        P(None, "pipe", None, "expert"),
        P(None, "pipe", "expert", None),
        P(None, None, "pipe", "expert", None),
    )
    out_specs = P(None, "pipe", "expert", None)
    return jax.shard_map(shards, mesh=mesh, in_specs=in_specs, out_specs=out_specs, check_vma=False)
```
